32 devices in a mesh: feat: 8 (over z, y), tok: 4 (over x, core).
Axes of the slice: x: 2, y: 2, z: 4, core: 2. Of those that a mesh axis runs over, the one named last changes fastest.
Arguments:
- activations: bfloat16 [2048, 7168], P('tok', 'feat'), may hold values from -6 to 6
- top_lists: int32 [2048, 64], P('tok'), may hold values from 0 to 4095, all different within a row
- encoder_weight: bfloat16 [7168, 4096], P(None, 'feat'), may hold values from -0.0625 to 0.0625
- encoder_bias: float32 [4096], P('feat'), may hold values from -3 to 3
- decoder_weight: bfloat16 [7168, 4096], P(None, 'feat'), may hold values from -0.125 to 0.125
- decoder_bias: float32 [7168], replicated, may hold values from -3 to 3
Outputs:
- encoder_grad: float32 [7168, 4096], P('tok', 'feat')
- decoder_grad: float32 [7168, 4096], P('tok', 'feat')
The draws below stay inside these ranges and needn't reach their ends.
All inputs are finite; a program needn't handle non-finite values.
Results may differ from the reference program's by a relative error of at most 0.004.
Values may be sent and summed in bfloat16 or wider, within the bound.
A program may use at most 128 MiB of HBM per device.

```python
import jax
import jax.numpy as jnp
from jax import lax

D = 3584
TOPK = 64
FEATURES = 4096
TOKENS = 2048


def block_levels(own_key, dims, cuts, low, top_value):
    level, own = 1.0, jax.random.fold_in(own_key, 6)
    for position, shards_of in cuts:
        steps = jnp.exp(jax.random.uniform(jax.random.fold_in(own, position), (shards_of,), jnp.float32, low / len(cuts), top_value / len(cuts)))
        level = level * jnp.repeat(steps, dims[position] // shards_of).reshape([-1 if axis == position else 1 for axis in range(len(dims))])
    return level


def distinct(stream_key, rows, number_of, top, lift):
    sequence = jax.random.permutation(jax.random.fold_in(stream_key, 1), number_of)
    favour = sequence
    for power in range(3):
        favour = favour * favour // number_of
    favour = favour * lift // number_of
    lots = jax.random.randint(jax.random.fold_in(stream_key, 2), (rows, number_of), 0, 4096) + favour
    sure = jax.random.permutation(jax.random.fold_in(stream_key, 3), rows)[jnp.arange(number_of) % rows]
    lots = jnp.where(jnp.arange(rows)[:, None] == sure[None, :], 1 << 14, lots)
    merit = lots * number_of + jnp.arange(number_of)
    return lax.top_k(merit.astype(jnp.int32), top)[1].astype(jnp.int32)


def gaussian(rng, extent, deviation, most, cuts=(), kind=jnp.bfloat16):
    entries = jax.random.normal(rng, extent, jnp.float32) * deviation
    if len(cuts) > 0:
        entries = block_levels(rng, extent, cuts, -0.22, 0.18) * entries
    return jnp.clip(entries, min=-most, max=most).astype(kind)


def setup_inputs(seed: int = 0) -> dict:
    key_of = jax.random.split(jax.random.key(seed), 7)
    return {
        "activations": gaussian(key_of[0], (TOKENS, 2 * D), 1.0, 6.0, ((0, 4), (1, 8))),
        "top_lists": distinct(key_of[1], TOKENS, FEATURES, TOPK, 256),
        "encoder_weight": gaussian(key_of[2], (2 * D, FEATURES), (2 * D) ** -0.5, 0.0625, ((1, 8),)),
        "encoder_bias": gaussian(key_of[3], (FEATURES,), 0.5, 3.0, ((0, 8),), jnp.float32),
        "decoder_weight": gaussian(key_of[4], (2 * D, FEATURES), (32 * TOPK) ** -0.5, 0.125, ((1, 8),)),
        "decoder_bias": gaussian(key_of[5], (2 * D,), 0.5, 3.0, (), jnp.float32),
    }


def contract_rows(left, right):
    return lax.dot_general(left, right, (((0,), (0,)), ((), ())), preferred_element_type=jnp.float32)


def reference(activations, top_lists, encoder_weight, encoder_bias, decoder_weight, decoder_bias):
    token_count = activations.shape[0]
    encoded = jnp.dot(activations, encoder_weight, preferred_element_type=jnp.float32) + encoder_bias
    row_ids = jnp.arange(token_count, dtype=jnp.int32)[:, None]
    chosen = jnp.zeros(encoded.shape, jnp.float32).at[row_ids, top_lists].set(1.0)
    codes = jnp.where(chosen > 0.0, encoded, 0.0).astype(jnp.bfloat16)
    rebuilt = lax.dot_general(codes, decoder_weight, (((1,), (1,)), ((), ())), preferred_element_type=jnp.float32)
    error = (rebuilt + decoder_bias - activations.astype(jnp.float32)).astype(jnp.bfloat16)
    pulled = jnp.dot(error, decoder_weight, preferred_element_type=jnp.float32)
    code_grads = jnp.where(chosen > 0.0, pulled, 0.0).astype(jnp.bfloat16)
    encoder_grad = contract_rows(activations, code_grads)
    decoder_grad = contract_rows(error, codes)
    return encoder_grad, decoder_grad
```

```python
import functools

import jax
import jax.numpy as jnp
from jax import lax
from jax.experimental import pallas as pl
from jax.experimental.pallas import tpu as pltpu
from jax.sharding import PartitionSpec as P

ROWS = 128


def pick(values, lanes):
    return jnp.take_along_axis(values, lanes, axis=1, mode="promise_in_bounds")


def place_kernel(width, ids_ref, out_ref):
    rows, top = ids_ref.shape[1:]
    chunks = out_ref.shape[2] // width
    base = pl.program_id(0) * top
    lane = lax.broadcasted_iota(jnp.int32, (8, width), 1)

    def group(step, carry):
        at = pl.ds(pl.multiple_of(step * 8, 8), 8)
        ids = ids_ref[0, at, :]
        found = [jnp.full((8, width), -1, jnp.int32)] * chunks
        for k in range(top):
            relative = jnp.broadcast_to(ids[:, k : k + 1], (8, width)) - lane
            found = [jnp.where(relative == c * width, k, found[c]) for c in range(chunks)]
        for c in range(chunks):
            out_ref[0, at, c * width : (c + 1) * width] = jnp.where(
                found[c] >= 0, found[c] + base, -1
            )
        return carry

    lax.fori_loop(0, rows // 8, group, 0)


def place(ids, features, width):
    packs, rows, top = ids.shape
    return pl.pallas_call(
        functools.partial(place_kernel, width),
        grid=(packs, rows // ROWS),
        in_specs=[pl.BlockSpec((1, ROWS, top), lambda h, i: (h, i, 0))],
        out_specs=pl.BlockSpec((1, ROWS, features), lambda h, i: (h, i, 0)),
        out_shape=jax.ShapeDtypeStruct((packs, rows, features), jnp.int32),
        cost_estimate=pl.CostEstimate(
            flops=packs * rows * top * features * 20, bytes_accessed=packs * rows * features * 4,
            transcendentals=0,
        ),
        name="place",
    )(ids)


def project_kernel(width, rows_ref, weight_ref, ids_ref, bias_ref, out_ref):
    packs, rows, depth = rows_ref.shape
    chunks = weight_ref.shape[1] // width
    total = jnp.zeros((rows, width), jnp.float32)
    for h in range(packs):
        ids = ids_ref[h]
        chunk = lax.shift_right_arithmetic(ids, width.bit_length() - 1)
        lanes = lax.bitwise_and(ids, width - 1)
        for pair in range(0, chunks, 2):
            cols = slice(pair * width, (pair + 2) * width)
            product = jnp.dot(
                rows_ref[h], weight_ref[:, cols], preferred_element_type=jnp.float32
            ) + bias_ref[:, cols]
            for c in range(2):
                got = pick(product[:, c * width : (c + 1) * width], lanes)
                total = jnp.where(chunk == pair + c, got, total)
    out_ref[...] = total


def project(rows, weight, ids, bias, width):
    packs, count, depth = rows.shape
    features = weight.shape[1]
    return pl.pallas_call(
        functools.partial(project_kernel, width),
        grid=(count // ROWS,),
        in_specs=[
            pl.BlockSpec((packs, ROWS, depth), lambda i: (0, i, 0)),
            pl.BlockSpec((depth, features), lambda i: (0, 0)),
            pl.BlockSpec((packs, ROWS, width), lambda i: (0, i, 0)),
            pl.BlockSpec((1, features), lambda i: (0, 0)),
        ],
        out_specs=pl.BlockSpec((ROWS, width), lambda i: (i, 0)),
        out_shape=jax.ShapeDtypeStruct((count, width), jnp.float32),
        cost_estimate=pl.CostEstimate(
            flops=2 * packs * count * depth * features,
            bytes_accessed=rows.size * 2 + weight.size * 2, transcendentals=0,
        ),
        name="project",
    )(rows, weight, ids, bias)


def spread_kernel(width, packed_ref, place_ref, out_ref):
    packed = packed_ref[...]
    for h in range(place_ref.shape[0]):
        for c in range(place_ref.shape[2] // width):
            cols = slice(c * width, (c + 1) * width)
            at = place_ref[h, :, cols]
            got = pick(packed, jnp.maximum(at, 0))
            out_ref[h, :, cols] = jnp.where(at >= 0, got, 0.0).astype(jnp.bfloat16)


def spread(packed, places):
    packs, count, features = places.shape
    width = packed.shape[1]
    return pl.pallas_call(
        functools.partial(spread_kernel, width),
        grid=(count // ROWS,),
        in_specs=[
            pl.BlockSpec((ROWS, width), lambda i: (i, 0)),
            pl.BlockSpec((packs, ROWS, features), lambda i: (0, i, 0)),
        ],
        out_specs=pl.BlockSpec((packs, ROWS, features), lambda i: (0, i, 0)),
        out_shape=jax.ShapeDtypeStruct(places.shape, jnp.bfloat16),
        cost_estimate=pl.CostEstimate(
            flops=places.size * 4, bytes_accessed=places.size * 6, transcendentals=0
        ),
        name="spread",
    )(packed, places)


def contract_rows(left, right):
    return lax.dot_general(
        left, right, (((0,), (0,)), ((), ())), preferred_element_type=jnp.float32
    )


def body(activations, top_lists, encoder_weight, encoder_bias, decoder_weight, decoder_bias):
    group_rows, hidden_dev = activations.shape
    feat_dev = encoder_weight.shape[1]
    top = top_lists.shape[1]
    shards, groups = lax.axis_size("feat"), lax.axis_size("tok")
    owner, group = lax.axis_index("feat"), lax.axis_index("tok")
    width = feat_dev // groups
    features = shards * width
    packs = width // top
    all_rows = group_rows * groups

    def own_weight(weight):
        columns = lax.dynamic_slice_in_dim(weight, group * width, width, 1)
        return lax.all_to_all(columns, "feat", split_axis=0, concat_axis=1, tiled=True)

    lists = lax.all_gather(top_lists, "tok", axis=0, tiled=True)
    inputs = lax.all_gather(activations, "tok", axis=0, tiled=True)
    encoder_own = own_weight(encoder_weight)
    decoder_own = own_weight(decoder_weight)

    in_block = lists % feat_dev
    local = jnp.where(
        in_block // width == group, lists // feat_dev * width + in_block % width, -1
    ).reshape(packs, all_rows // packs, top)
    packed_ids = jnp.stack(
        [
            jnp.pad(local[h], ((0, 0), (h * top, width - (h + 1) * top)), constant_values=-1)
            for h in range(packs)
        ]
    )
    places = place(local, features, width)
    bias = lax.dynamic_update_slice(
        jnp.zeros((1, features), jnp.float32),
        lax.dynamic_slice_in_dim(encoder_bias, group * width, width)[None, :],
        (0, owner * width),
    )

    def project_sum(rows, weight, offset):
        part = project(rows.reshape(packs, all_rows // packs, hidden_dev), weight, packed_ids, offset, width)
        return spread(lax.psum(part, "feat"), places).reshape(all_rows, features)

    codes = project_sum(inputs, encoder_own, bias)
    rebuilt = lax.psum_scatter(
        lax.dot_general(
            codes, decoder_own, (((1,), (1,)), ((), ())), preferred_element_type=jnp.float32
        ).astype(jnp.bfloat16),
        "tok",
        scatter_dimension=0,
        tiled=True,
    )
    own_bias = lax.dynamic_slice_in_dim(decoder_bias, owner * hidden_dev, hidden_dev)
    error_rows = (
        rebuilt.astype(jnp.float32) + own_bias - activations.astype(jnp.float32)
    ).astype(jnp.bfloat16)
    error = lax.all_gather(error_rows, "tok", axis=0, tiled=True)

    def send_home(gradient):
        tall = lax.all_to_all(gradient, "feat", split_axis=1, concat_axis=0, tiled=True)
        return lax.all_to_all(tall, "tok", split_axis=0, concat_axis=1, tiled=True)

    code_grads = project_sum(error, decoder_own, jnp.zeros_like(bias))
    decoder_grad = send_home(contract_rows(error, codes).astype(jnp.bfloat16))
    encoder_grad = send_home(contract_rows(inputs, code_grads).astype(jnp.bfloat16))
    return (encoder_grad.astype(jnp.float32), decoder_grad.astype(jnp.float32))


def solution(mesh):
    return jax.shard_map(
        body,
        mesh=mesh,
        in_specs=(
            P("tok", "feat"),
            P("tok", None),
            P(None, "feat"),
            P("feat"),
            P(None, "feat"),
            P(),
        ),
        out_specs=(P("tok", "feat"), P("tok", "feat")),
        check_vma=False,
    )
```

```python
import functools

import jax
import jax.numpy as jnp
from jax import lax
from jax.experimental import pallas as pl
from jax.experimental.pallas import tpu as pltpu
from jax.sharding import PartitionSpec as P

ROWS = 128


def pick(values, lanes):
    return jnp.take_along_axis(values, lanes, axis=1, mode="promise_in_bounds")


def place_kernel(width, ids_ref, out_ref):
    rows, top = ids_ref.shape[1:]
    chunks = out_ref.shape[2] // width
    base = pl.program_id(0) * top
    lane = lax.broadcasted_iota(jnp.int32, (8, width), 1)

    def group(step, carry):
        at = pl.ds(pl.multiple_of(step * 8, 8), 8)
        ids = ids_ref[0, at, :]
        found = [jnp.full((8, width), -1, jnp.int32)] * chunks
        for k in range(top):
            relative = jnp.broadcast_to(ids[:, k : k + 1], (8, width)) - lane
            found = [jnp.where(relative == c * width, k, found[c]) for c in range(chunks)]
        for c in range(chunks):
            out_ref[0, at, c * width : (c + 1) * width] = jnp.where(
                found[c] >= 0, found[c] + base, -1
            )
        return carry

    lax.fori_loop(0, rows // 8, group, 0)


def place(ids, features, width):
    packs, rows, top = ids.shape
    return pl.pallas_call(
        functools.partial(place_kernel, width),
        grid=(packs, rows // ROWS),
        in_specs=[pl.BlockSpec((1, ROWS, top), lambda h, i: (h, i, 0))],
        out_specs=pl.BlockSpec((1, ROWS, features), lambda h, i: (h, i, 0)),
        out_shape=jax.ShapeDtypeStruct((packs, rows, features), jnp.int32),
        cost_estimate=pl.CostEstimate(
            flops=packs * rows * top * features * 20, bytes_accessed=packs * rows * features * 4,
            transcendentals=0,
        ),
        name="place",
    )(ids)


def project_kernel(width, rows_ref, weight_ref, ids_ref, bias_ref, out_ref):
    packs, rows, depth = rows_ref.shape
    chunks = weight_ref.shape[1] // width
    total = jnp.zeros((rows, width), jnp.float32)
    for h in range(packs):
        ids = ids_ref[h]
        chunk = lax.shift_right_arithmetic(ids, width.bit_length() - 1)
        lanes = lax.bitwise_and(ids, width - 1)
        for pair in range(0, chunks, 2):
            cols = slice(pair * width, (pair + 2) * width)
            product = jnp.dot(
                rows_ref[h], weight_ref[:, cols], preferred_element_type=jnp.float32
            ) + bias_ref[:, cols]
            for c in range(2):
                got = pick(product[:, c * width : (c + 1) * width], lanes)
                total = jnp.where(chunk == pair + c, got, total)
    out_ref[...] = total


def project(rows, weight, ids, bias, width):
    packs, count, depth = rows.shape
    features = weight.shape[1]
    return pl.pallas_call(
        functools.partial(project_kernel, width),
        grid=(count // ROWS,),
        in_specs=[
            pl.BlockSpec((packs, ROWS, depth), lambda i: (0, i, 0)),
            pl.BlockSpec((depth, features), lambda i: (0, 0)),
            pl.BlockSpec((packs, ROWS, width), lambda i: (0, i, 0)),
            pl.BlockSpec((1, features), lambda i: (0, 0)),
        ],
        out_specs=pl.BlockSpec((ROWS, width), lambda i: (i, 0)),
        out_shape=jax.ShapeDtypeStruct((count, width), jnp.float32),
        cost_estimate=pl.CostEstimate(
            flops=2 * packs * count * depth * features,
            bytes_accessed=rows.size * 2 + weight.size * 2, transcendentals=0,
        ),
        name="project",
    )(rows, weight, ids, bias)


def spread_kernel(width, packed_ref, place_ref, out_ref):
    packed = packed_ref[...].astype(jnp.float32)
    for h in range(place_ref.shape[0]):
        for c in range(place_ref.shape[2] // width):
            cols = slice(c * width, (c + 1) * width)
            at = place_ref[h, :, cols]
            got = pick(packed, jnp.maximum(at, 0))
            out_ref[h, :, cols] = jnp.where(at >= 0, got, 0.0).astype(jnp.bfloat16)


def spread(packed, places):
    packs, count, features = places.shape
    width = packed.shape[1]
    return pl.pallas_call(
        functools.partial(spread_kernel, width),
        grid=(count // ROWS,),
        in_specs=[
            pl.BlockSpec((ROWS, width), lambda i: (i, 0)),
            pl.BlockSpec((packs, ROWS, features), lambda i: (0, i, 0)),
        ],
        out_specs=pl.BlockSpec((packs, ROWS, features), lambda i: (0, i, 0)),
        out_shape=jax.ShapeDtypeStruct(places.shape, jnp.bfloat16),
        cost_estimate=pl.CostEstimate(
            flops=places.size * 4, bytes_accessed=places.size * 6, transcendentals=0
        ),
        name="spread",
    )(packed, places)


def join_kernel(width, me_ref, own_ref, *refs):
    *came_refs, out_ref = refs
    groups = len(came_refs) + 1
    for step, came in enumerate((own_ref, *came_refs)):
        source = lax.rem(me_ref[0] + groups - step, groups)
        at = pl.ds(pl.multiple_of(source * width, width), width)
        out_ref[:, at] = came[...].astype(jnp.float32)


def join(group, tall, came):
    rows, width = came[0].shape
    groups = len(came) + 1
    tile = rows // 4
    return pl.pallas_call(
        functools.partial(join_kernel, width),
        grid_spec=pltpu.PrefetchScalarGridSpec(
            num_scalar_prefetch=1,
            grid=(rows // tile,),
            in_specs=[
                pl.BlockSpec((tile, width), lambda i, me: (me[0] * (rows // tile) + i, 0)),
                *[pl.BlockSpec((tile, width), lambda i, me: (i, 0))] * len(came),
            ],
            out_specs=pl.BlockSpec((tile, groups * width), lambda i, me: (i, 0)),
        ),
        out_shape=jax.ShapeDtypeStruct((rows, groups * width), jnp.float32),
        cost_estimate=pl.CostEstimate(
            flops=rows * groups * width, bytes_accessed=rows * groups * width * 6, transcendentals=0
        ),
        name="join",
    )(group[None], tall, *came)


def contract_rows(left, right):
    return lax.dot_general(
        left, right, (((0,), (0,)), ((), ())), preferred_element_type=jnp.float32
    )


def body(activations, top_lists, encoder_weight, encoder_bias, decoder_weight, decoder_bias):
    group_rows, hidden_dev = activations.shape
    feat_dev = encoder_weight.shape[1]
    top = top_lists.shape[1]
    shards, groups = lax.axis_size("feat"), lax.axis_size("tok")
    owner, group = lax.axis_index("feat"), lax.axis_index("tok")
    width = feat_dev // groups
    features = shards * width
    packs = width // top
    all_rows = group_rows * groups

    def own_columns(weight):
        return lax.dynamic_slice_in_dim(weight, group * width, width, 1)

    def own_weight(columns):
        return lax.all_to_all(columns, "feat", split_axis=0, concat_axis=1, tiled=True)

    lists = lax.all_gather(top_lists, "tok", axis=0, tiled=True)
    inputs = lax.all_gather(activations, "tok", axis=0, tiled=True)
    encoder_columns, lists = lax.optimization_barrier((own_columns(encoder_weight), lists))
    encoder_own = own_weight(encoder_columns)

    in_block = lists % feat_dev
    local = jnp.where(
        in_block // width == group, lists // feat_dev * width + in_block % width, -1
    ).reshape(packs, all_rows // packs, top)
    packed_ids = jnp.stack(
        [
            jnp.pad(local[h], ((0, 0), (h * top, width - (h + 1) * top)), constant_values=-1)
            for h in range(packs)
        ]
    )
    places = place(local, features, width)
    encoder_own, places = lax.optimization_barrier((encoder_own, places))
    decoder_columns, encoder_own = lax.optimization_barrier((own_columns(decoder_weight), encoder_own))
    decoder_own = own_weight(decoder_columns)
    bias = lax.dynamic_update_slice(
        jnp.zeros((1, features), jnp.float32),
        lax.dynamic_slice_in_dim(encoder_bias, group * width, width)[None, :],
        (0, owner * width),
    )

    def project_sum(rows, weight, offset):
        part = project(rows.reshape(packs, all_rows // packs, hidden_dev), weight, packed_ids, offset, width)
        terms = lax.all_to_all(
            part.reshape(shards, -1, width), "feat", split_axis=0, concat_axis=0, tiled=True
        )
        share = jnp.sum(terms, axis=0).astype(jnp.bfloat16)
        return spread(lax.all_gather(share, "feat", axis=0, tiled=True), places).reshape(all_rows, features)

    codes = project_sum(inputs, encoder_own, bias)
    rebuilt = lax.psum_scatter(
        lax.dot_general(
            codes, decoder_own, (((1,), (1,)), ((), ())), preferred_element_type=jnp.float32
        ).astype(jnp.bfloat16),
        "tok",
        scatter_dimension=0,
        tiled=True,
    )
    own_bias = lax.dynamic_slice_in_dim(decoder_bias, owner * hidden_dev, hidden_dev)
    error_rows = (
        rebuilt.astype(jnp.float32) + own_bias - activations.astype(jnp.float32)
    ).astype(jnp.bfloat16)
    error = lax.all_gather(error_rows, "tok", axis=0, tiled=True)

    def send_home(gradient):
        tall = lax.all_to_all(
            gradient.astype(jnp.bfloat16), "feat", split_axis=1, concat_axis=0, tiled=True
        )
        rows = tall.shape[0] // groups
        came = []
        for step in range(1, groups):
            target = lax.rem(group + step, groups)
            block = lax.dynamic_slice_in_dim(tall, target * rows, rows, 0)
            ring = [(g, (g + step) % groups) for g in range(groups)]
            came.append(lax.ppermute(block, "tok", ring))
        return join(group, tall, came)

    code_grads = project_sum(error, decoder_own, jnp.zeros_like(bias))
    decoder_grad = send_home(contract_rows(error, codes))
    encoder_grad = send_home(contract_rows(inputs, code_grads))
    return (encoder_grad, decoder_grad)


def solution(mesh):
    return jax.shard_map(
        body,
        mesh=mesh,
        in_specs=(
            P("tok", "feat"),
            P("tok", None),
            P(None, "feat"),
            P("feat"),
            P(None, "feat"),
            P(),
        ),
        out_specs=(P("tok", "feat"), P("tok", "feat")),
        check_vma=False,
    )
```

```python
import functools

import jax
import jax.numpy as jnp
from jax import lax
from jax.experimental import pallas as pl
from jax.experimental.pallas import tpu as pltpu
from jax.sharding import PartitionSpec as P

ROWS = 128


def pick(values, lanes):
    return jnp.take_along_axis(values, lanes, axis=1, mode="promise_in_bounds")


def place_kernel(width, ids_ref, out_ref):
    rows, top = ids_ref.shape[1:]
    chunks = out_ref.shape[2] // width
    base = pl.program_id(0) * top
    lane = lax.broadcasted_iota(jnp.int32, (8, width), 1)

    def group(step, carry):
        at = pl.ds(pl.multiple_of(step * 8, 8), 8)
        ids = ids_ref[0, at, :]
        found = [jnp.full((8, width), -1, jnp.int32)] * chunks
        for k in range(top):
            relative = jnp.broadcast_to(ids[:, k : k + 1], (8, width)) - lane
            found = [jnp.where(relative == c * width, k, found[c]) for c in range(chunks)]
        for c in range(chunks):
            out_ref[0, at, c * width : (c + 1) * width] = jnp.where(
                found[c] >= 0, found[c] + base, -1
            )
        return carry

    lax.fori_loop(0, rows // 8, group, 0)


def place(ids, features, width):
    packs, rows, top = ids.shape
    return pl.pallas_call(
        functools.partial(place_kernel, width),
        grid=(packs, rows // ROWS),
        in_specs=[pl.BlockSpec((1, ROWS, top), lambda h, i: (h, i, 0))],
        out_specs=pl.BlockSpec((1, ROWS, features), lambda h, i: (h, i, 0)),
        out_shape=jax.ShapeDtypeStruct((packs, rows, features), jnp.int32),
        cost_estimate=pl.CostEstimate(
            flops=packs * rows * top * features * 20, bytes_accessed=packs * rows * features * 4,
            transcendentals=0,
        ),
        name="place",
    )(ids)


def project_kernel(width, rows_ref, weight_ref, ids_ref, bias_ref, out_ref):
    packs, rows, depth = rows_ref.shape
    chunks = weight_ref.shape[1] // width
    total = jnp.zeros((rows, width), jnp.float32)
    for h in range(packs):
        ids = ids_ref[h]
        chunk = lax.shift_right_arithmetic(ids, width.bit_length() - 1)
        lanes = lax.bitwise_and(ids, width - 1)
        for pair in range(0, chunks, 2):
            cols = slice(pair * width, (pair + 2) * width)
            product = jnp.dot(
                rows_ref[h], weight_ref[:, cols], preferred_element_type=jnp.float32
            ) + bias_ref[:, cols]
            for c in range(2):
                got = pick(product[:, c * width : (c + 1) * width], lanes)
                total = jnp.where(chunk == pair + c, got, total)
    out_ref[...] = total


def project(rows, weight, ids, bias, width):
    packs, count, depth = rows.shape
    features = weight.shape[1]
    return pl.pallas_call(
        functools.partial(project_kernel, width),
        grid=(count // ROWS,),
        in_specs=[
            pl.BlockSpec((packs, ROWS, depth), lambda i: (0, i, 0)),
            pl.BlockSpec((depth, features), lambda i: (0, 0)),
            pl.BlockSpec((packs, ROWS, width), lambda i: (0, i, 0)),
            pl.BlockSpec((1, features), lambda i: (0, 0)),
        ],
        out_specs=pl.BlockSpec((ROWS, width), lambda i: (i, 0)),
        out_shape=jax.ShapeDtypeStruct((count, width), jnp.float32),
        cost_estimate=pl.CostEstimate(
            flops=2 * packs * count * depth * features,
            bytes_accessed=rows.size * 2 + weight.size * 2, transcendentals=0,
        ),
        name="project",
    )(rows, weight, ids, bias)


def spread_kernel(width, packed_ref, place_ref, out_ref):
    packed = packed_ref[...].astype(jnp.float32)
    for h in range(place_ref.shape[0]):
        for c in range(place_ref.shape[2] // width):
            cols = slice(c * width, (c + 1) * width)
            at = place_ref[h, :, cols]
            got = pick(packed, jnp.maximum(at, 0))
            out_ref[h, :, cols] = jnp.where(at >= 0, got, 0.0).astype(jnp.bfloat16)


def spread(packed, places):
    packs, count, features = places.shape
    width = packed.shape[1]
    return pl.pallas_call(
        functools.partial(spread_kernel, width),
        grid=(count // ROWS,),
        in_specs=[
            pl.BlockSpec((ROWS, width), lambda i: (i, 0)),
            pl.BlockSpec((packs, ROWS, features), lambda i: (0, i, 0)),
        ],
        out_specs=pl.BlockSpec((packs, ROWS, features), lambda i: (0, i, 0)),
        out_shape=jax.ShapeDtypeStruct(places.shape, jnp.bfloat16),
        cost_estimate=pl.CostEstimate(
            flops=places.size * 4, bytes_accessed=places.size * 6, transcendentals=0
        ),
        name="spread",
    )(packed, places)


def join_kernel(width, me_ref, own_ref, *refs):
    *came_refs, out_ref = refs
    groups = len(came_refs) + 1
    for step, came in enumerate((own_ref, *came_refs)):
        source = lax.rem(me_ref[0] + groups - step, groups)
        at = pl.ds(pl.multiple_of(source * width, width), width)
        out_ref[:, at] = came[...].astype(jnp.float32)


def join(group, tall, came):
    rows, width = came[0].shape
    groups = len(came) + 1
    tile = rows // 4
    return pl.pallas_call(
        functools.partial(join_kernel, width),
        grid_spec=pltpu.PrefetchScalarGridSpec(
            num_scalar_prefetch=1,
            grid=(rows // tile,),
            in_specs=[
                pl.BlockSpec((tile, width), lambda i, me: (me[0] * (rows // tile) + i, 0)),
                *[pl.BlockSpec((tile, width), lambda i, me: (i, 0))] * len(came),
            ],
            out_specs=pl.BlockSpec((tile, groups * width), lambda i, me: (i, 0)),
        ),
        out_shape=jax.ShapeDtypeStruct((rows, groups * width), jnp.float32),
        cost_estimate=pl.CostEstimate(
            flops=rows * groups * width, bytes_accessed=rows * groups * width * 6, transcendentals=0
        ),
        name="join",
    )(group[None], tall, *came)


def contract_rows(left, right):
    return lax.dot_general(
        left, right, (((0,), (0,)), ((), ())), preferred_element_type=jnp.float32
    )


def body(activations, top_lists, encoder_weight, encoder_bias, decoder_weight, decoder_bias):
    group_rows, hidden_dev = activations.shape
    feat_dev = encoder_weight.shape[1]
    top = top_lists.shape[1]
    shards, groups = lax.axis_size("feat"), lax.axis_size("tok")
    owner, group = lax.axis_index("feat"), lax.axis_index("tok")
    width = feat_dev // groups
    features = shards * width
    packs = width // top
    all_rows = group_rows * groups

    def own_columns(weight):
        return lax.dynamic_slice_in_dim(weight, group * width, width, 1)

    lists = lax.all_gather(top_lists, "tok", axis=0, tiled=True)
    inputs = lax.all_gather(activations, "tok", axis=0, tiled=True)
    both = jnp.concatenate([own_columns(encoder_weight), own_columns(decoder_weight)], axis=1)
    arrived = lax.all_to_all(
        both.reshape(shards, hidden_dev, 2 * width), "feat", split_axis=0, concat_axis=0, tiled=True
    )

    in_block = lists % feat_dev
    local = jnp.where(
        in_block // width == group, lists // feat_dev * width + in_block % width, -1
    ).reshape(packs, all_rows // packs, top)
    packed_ids = jnp.stack(
        [
            jnp.pad(local[h], ((0, 0), (h * top, width - (h + 1) * top)), constant_values=-1)
            for h in range(packs)
        ]
    )
    places = place(local, features, width)
    arrived, places = lax.optimization_barrier((arrived, places))
    encoder_own, decoder_own = (
        arrived[:, :, at : at + width].transpose(1, 0, 2).reshape(hidden_dev, features)
        for at in (0, width)
    )
    bias = lax.dynamic_update_slice(
        jnp.zeros((1, features), jnp.float32),
        lax.dynamic_slice_in_dim(encoder_bias, group * width, width)[None, :],
        (0, owner * width),
    )

    def packed_sum(rows, weight, offset):
        part = project(rows.reshape(packs, all_rows // packs, hidden_dev), weight, packed_ids, offset, width)
        terms = lax.all_to_all(
            part.reshape(shards, -1, width), "feat", split_axis=0, concat_axis=0, tiled=True
        )
        share = jnp.sum(terms, axis=0).astype(jnp.bfloat16)
        return lax.all_gather(share, "feat", axis=0, tiled=True)

    def spread_rows(packed):
        return spread(packed, places).reshape(all_rows, features)

    codes = spread_rows(packed_sum(inputs, encoder_own, bias))
    rebuilt = lax.psum_scatter(
        lax.dot_general(
            codes, decoder_own, (((1,), (1,)), ((), ())), preferred_element_type=jnp.float32
        ).astype(jnp.bfloat16),
        "tok",
        scatter_dimension=0,
        tiled=True,
    )
    own_bias = lax.dynamic_slice_in_dim(decoder_bias, owner * hidden_dev, hidden_dev)
    error_rows = (
        rebuilt.astype(jnp.float32) + own_bias - activations.astype(jnp.float32)
    ).astype(jnp.bfloat16)
    error = lax.all_gather(error_rows, "tok", axis=0, tiled=True)

    def send_home(gradient):
        tall = lax.all_to_all(
            gradient, "feat", split_axis=1, concat_axis=0, tiled=True
        )
        rows = tall.shape[0] // groups
        came = []
        for step in range(1, groups):
            target = lax.rem(group + step, groups)
            block = lax.dynamic_slice_in_dim(tall, target * rows, rows, 0)
            ring = [(g, (g + step) % groups) for g in range(groups)]
            came.append(lax.ppermute(block, "tok", ring))
        return join(group, tall, came)

    packed_grads, decoder_part = lax.optimization_barrier(
        (
            packed_sum(error, decoder_own, jnp.zeros_like(bias)),
            contract_rows(error, codes).astype(jnp.bfloat16),
        )
    )
    decoder_grad = send_home(decoder_part)
    code_grads = spread_rows(packed_grads)
    encoder_grad = send_home(contract_rows(inputs, code_grads).astype(jnp.bfloat16))
    return (encoder_grad, decoder_grad)


def solution(mesh):
    return jax.shard_map(
        body,
        mesh=mesh,
        in_specs=(
            P("tok", "feat"),
            P("tok", None),
            P(None, "feat"),
            P("feat"),
            P(None, "feat"),
            P(),
        ),
        out_specs=(P("tok", "feat"), P("tok", "feat")),
        check_vma=False,
    )
```

```python
import functools

import jax
import jax.numpy as jnp
from jax import lax
from jax.experimental import pallas as pl
from jax.experimental.pallas import tpu as pltpu
from jax.sharding import PartitionSpec as P

ROWS = 128


def pick(values, lanes):
    return jnp.take_along_axis(values, lanes, axis=1, mode="promise_in_bounds")


def place_kernel(width, ids_ref, out_ref):
    rows, top = ids_ref.shape[1:]
    chunks = out_ref.shape[2] // width
    base = pl.program_id(0) * top
    lane = lax.broadcasted_iota(jnp.int32, (8, width), 1)

    def group(step, carry):
        at = pl.ds(pl.multiple_of(step * 8, 8), 8)
        ids = ids_ref[0, at, :]
        found = [jnp.full((8, width), -1, jnp.int32)] * chunks
        for k in range(top):
            relative = jnp.broadcast_to(ids[:, k : k + 1], (8, width)) - lane
            found = [jnp.where(relative == c * width, k, found[c]) for c in range(chunks)]
        for c in range(chunks):
            out_ref[0, at, c * width : (c + 1) * width] = jnp.where(
                found[c] >= 0, found[c] + base, -1
            )
        return carry

    lax.fori_loop(0, rows // 8, group, 0)


def place(ids, features, width):
    packs, rows, top = ids.shape
    return pl.pallas_call(
        functools.partial(place_kernel, width),
        grid=(packs, rows // ROWS),
        in_specs=[pl.BlockSpec((1, ROWS, top), lambda h, i: (h, i, 0))],
        out_specs=pl.BlockSpec((1, ROWS, features), lambda h, i: (h, i, 0)),
        out_shape=jax.ShapeDtypeStruct((packs, rows, features), jnp.int32),
        cost_estimate=pl.CostEstimate(
            flops=packs * rows * top * features * 20, bytes_accessed=packs * rows * features * 4,
            transcendentals=0,
        ),
        name="place",
    )(ids)


def project_kernel(width, rows_ref, weight_ref, ids_ref, bias_ref, out_ref):
    packs, rows, depth = rows_ref.shape
    chunks = weight_ref.shape[1] // width
    total = jnp.zeros((rows, width), jnp.float32)
    for h in range(packs):
        ids = ids_ref[h]
        chunk = lax.shift_right_arithmetic(ids, width.bit_length() - 1)
        lanes = lax.bitwise_and(ids, width - 1)
        for pair in range(0, chunks, 2):
            cols = slice(pair * width, (pair + 2) * width)
            product = jnp.dot(
                rows_ref[h], weight_ref[:, cols], preferred_element_type=jnp.float32
            ) + bias_ref[:, cols]
            for c in range(2):
                got = pick(product[:, c * width : (c + 1) * width], lanes)
                total = jnp.where(chunk == pair + c, got, total)
    out_ref[...] = total


def project(rows, weight, ids, bias, width):
    packs, count, depth = rows.shape
    features = weight.shape[1]
    return pl.pallas_call(
        functools.partial(project_kernel, width),
        grid=(count // ROWS,),
        in_specs=[
            pl.BlockSpec((packs, ROWS, depth), lambda i: (0, i, 0)),
            pl.BlockSpec((depth, features), lambda i: (0, 0)),
            pl.BlockSpec((packs, ROWS, width), lambda i: (0, i, 0)),
            pl.BlockSpec((1, features), lambda i: (0, 0)),
        ],
        out_specs=pl.BlockSpec((ROWS, width), lambda i: (i, 0)),
        out_shape=jax.ShapeDtypeStruct((count, width), jnp.float32),
        cost_estimate=pl.CostEstimate(
            flops=2 * packs * count * depth * features,
            bytes_accessed=rows.size * 2 + weight.size * 2, transcendentals=0,
        ),
        name="project",
    )(rows, weight, ids, bias)


def spread_kernel(width, packed_ref, place_ref, out_ref):
    packed = packed_ref[...].astype(jnp.float32)
    for h in range(place_ref.shape[0]):
        for c in range(place_ref.shape[2] // width):
            cols = slice(c * width, (c + 1) * width)
            at = place_ref[h, :, cols]
            got = pick(packed, jnp.maximum(at, 0))
            out_ref[h, :, cols] = jnp.where(at >= 0, got, 0.0).astype(jnp.bfloat16)


def spread(packed, places):
    packs, count, features = places.shape
    width = packed.shape[1]
    return pl.pallas_call(
        functools.partial(spread_kernel, width),
        grid=(count // ROWS,),
        in_specs=[
            pl.BlockSpec((ROWS, width), lambda i: (i, 0)),
            pl.BlockSpec((packs, ROWS, features), lambda i: (0, i, 0)),
        ],
        out_specs=pl.BlockSpec((packs, ROWS, features), lambda i: (0, i, 0)),
        out_shape=jax.ShapeDtypeStruct(places.shape, jnp.bfloat16),
        cost_estimate=pl.CostEstimate(
            flops=places.size * 4, bytes_accessed=places.size * 6, transcendentals=0
        ),
        name="spread",
    )(packed, places)


def join_kernel(width, me_ref, own_ref, *refs):
    *came_refs, out_ref = refs
    groups = len(came_refs) + 1
    for step, came in enumerate((own_ref, *came_refs)):
        source = lax.rem(me_ref[0] + groups - step, groups)
        at = pl.ds(pl.multiple_of(source * width, width), width)
        out_ref[:, at] = came[...].astype(jnp.float32)


def join(group, tall, came):
    rows, width = came[0].shape
    groups = len(came) + 1
    tile = rows // 4
    return pl.pallas_call(
        functools.partial(join_kernel, width),
        grid_spec=pltpu.PrefetchScalarGridSpec(
            num_scalar_prefetch=1,
            grid=(rows // tile,),
            in_specs=[
                pl.BlockSpec((tile, width), lambda i, me: (me[0] * (rows // tile) + i, 0)),
                *[pl.BlockSpec((tile, width), lambda i, me: (i, 0))] * len(came),
            ],
            out_specs=pl.BlockSpec((tile, groups * width), lambda i, me: (i, 0)),
        ),
        out_shape=jax.ShapeDtypeStruct((rows, groups * width), jnp.float32),
        cost_estimate=pl.CostEstimate(
            flops=rows * groups * width, bytes_accessed=rows * groups * width * 6, transcendentals=0
        ),
        name="join",
    )(group[None], tall, *came)


def contract_rows(left, right):
    return lax.dot_general(
        left, right, (((0,), (0,)), ((), ())), preferred_element_type=jnp.float32
    )


def body(activations, top_lists, encoder_weight, encoder_bias, decoder_weight, decoder_bias):
    group_rows, hidden_dev = activations.shape
    feat_dev = encoder_weight.shape[1]
    top = top_lists.shape[1]
    shards, groups = lax.axis_size("feat"), lax.axis_size("tok")
    owner, group = lax.axis_index("feat"), lax.axis_index("tok")
    width = feat_dev // groups
    features = shards * width
    packs = width // top
    all_rows = group_rows * groups

    def own_columns(weight):
        return lax.dynamic_slice_in_dim(weight, group * width, width, 1)

    lists = lax.all_gather(top_lists, "tok", axis=0, tiled=True)
    inputs = lax.all_gather(activations, "tok", axis=0, tiled=True)
    both = jnp.concatenate([own_columns(encoder_weight), own_columns(decoder_weight)], axis=1)
    arrived = lax.all_to_all(
        both.reshape(shards, hidden_dev, 2 * width), "feat", split_axis=0, concat_axis=0, tiled=True
    )

    in_block = lists % feat_dev
    local = jnp.where(
        in_block // width == group, lists // feat_dev * width + in_block % width, -1
    ).reshape(packs, all_rows // packs, top)
    packed_ids = jnp.stack(
        [
            jnp.pad(local[h], ((0, 0), (h * top, width - (h + 1) * top)), constant_values=-1)
            for h in range(packs)
        ]
    )
    places = place(local, features, width)
    arrived, places = lax.optimization_barrier((arrived, places))
    encoder_own, decoder_own = (
        arrived[:, :, at : at + width].transpose(1, 0, 2).reshape(hidden_dev, features)
        for at in (0, width)
    )
    bias = lax.dynamic_update_slice(
        jnp.zeros((1, features), jnp.float32),
        lax.dynamic_slice_in_dim(encoder_bias, group * width, width)[None, :],
        (0, owner * width),
    )

    def packed_sum(rows, weight, offset):
        part = project(rows.reshape(packs, all_rows // packs, hidden_dev), weight, packed_ids, offset, width)
        terms = lax.all_to_all(
            part.reshape(shards, -1, width), "feat", split_axis=0, concat_axis=0, tiled=True
        )
        share = jnp.sum(terms, axis=0).astype(jnp.bfloat16)
        copies = jnp.broadcast_to(share, (shards, *share.shape))
        return lax.all_to_all(copies, "feat", split_axis=0, concat_axis=0, tiled=True).reshape(-1, width)

    def spread_rows(packed):
        return spread(packed, places).reshape(all_rows, features)

    codes = spread_rows(packed_sum(inputs, encoder_own, bias))
    rebuilt = lax.psum_scatter(
        lax.dot_general(
            codes, decoder_own, (((1,), (1,)), ((), ())), preferred_element_type=jnp.float32
        ).astype(jnp.bfloat16),
        "tok",
        scatter_dimension=0,
        tiled=True,
    )
    own_bias = lax.dynamic_slice_in_dim(decoder_bias, owner * hidden_dev, hidden_dev)
    error_rows = (
        rebuilt.astype(jnp.float32) + own_bias - activations.astype(jnp.float32)
    ).astype(jnp.bfloat16)
    error = lax.all_gather(error_rows, "tok", axis=0, tiled=True)

    def send_home(gradient):
        tall = lax.all_to_all(
            gradient, "feat", split_axis=1, concat_axis=0, tiled=True
        )
        rows = tall.shape[0] // groups
        came = []
        for step in range(1, groups):
            target = lax.rem(group + step, groups)
            block = lax.dynamic_slice_in_dim(tall, target * rows, rows, 0)
            ring = [(g, (g + step) % groups) for g in range(groups)]
            came.append(lax.ppermute(block, "tok", ring))
        return join(group, tall, came)

    packed_grads, decoder_part = lax.optimization_barrier(
        (
            packed_sum(error, decoder_own, jnp.zeros_like(bias)),
            contract_rows(error, codes).astype(jnp.bfloat16),
        )
    )
    decoder_grad = send_home(decoder_part)
    code_grads = spread_rows(packed_grads)
    encoder_grad = send_home(contract_rows(inputs, code_grads).astype(jnp.bfloat16))
    return (encoder_grad, decoder_grad)


def solution(mesh):
    return jax.shard_map(
        body,
        mesh=mesh,
        in_specs=(
            P("tok", "feat"),
            P("tok", None),
            P(None, "feat"),
            P("feat"),
            P(None, "feat"),
            P(),
        ),
        out_specs=(P("tok", "feat"), P("tok", "feat")),
        check_vma=False,
    )
```
